32 devices in a mesh: dp: 4 (over y, x), shard: 4 (over z), rep: 2 (over core).
Axes of the slice: x: 2, y: 2, z: 4, core: 2. Of those that a mesh axis runs over, the one named last changes fastest.
Arguments:
- earlier_precise_parameters: float32 [8, 512, 128], P(('dp', 'rep'), 'shard'), may hold values from -6 to 6
- earlier_mean_estimate: float32 [8, 512, 128], P(('dp', 'rep'), 'shard'), may hold values from -6 to 6
- earlier_variance_estimate: float32 [8, 512, 128], P(('dp', 'rep'), 'shard'), may hold values from 0.01 to 10
- replica_slope_portions: bfloat16 [8, 8192, 128], P(('dp', 'rep'), 'shard'), may hold values from -6 to 6
- segment_fresh_owner: int32 [4, 4], replicated, may hold values from 0 to 3, as said below
- segment_line_lengths: int32 [4, 4], replicated, may hold values from 0 to 64, as said below
- remaining_worker: int32 [4], replicated, may hold values from 0 to 3, each once
Outputs:
- master_new: float32 [8, 1024, 128], P(('dp', 'rep'), 'shard')
- moment_new: float32 [8, 1024, 128], P(('dp', 'rep'), 'shard')
- second_new: float32 [8, 1024, 128], P(('dp', 'rep'), 'shard')
The draws below stay inside these ranges and needn't reach their ends.
Inputs may be any that keep to these rules, and one draw needn't show every extreme that they name: `segment_fresh_owner`: each row lists every new owner once. `segment_line_lengths`: each row sums to 128; one new owner, drawn anew, receives exactly 64 rows from every old rank, 256 in all; the blocks of any other owner hold at most 256 rows over all old ranks. `remaining_worker`: each old rank once.
All inputs are finite; a program needn't handle non-finite values.
Results may differ from the reference program's by a relative error of at most 0.0003.
Values sent between devices are 32-bit elements; how exact they have to be, the bound alone decides.
No kernel may reach another device: no remote copies, remote signals or barrier semaphores. Data moves between devices by JAX's collectives and lax.ppermute only.
A program may use at most 64 MiB of HBM per device.

```python
import math
import jax
import jax.numpy as jnp
from jax import lax

ROW_VALUES = 128
OLD_ROWS = 128
NEW_CAP = 256
GROUPS = 8
N_SHARD = 4


def plan_counts(key):
    count = N_SHARD
    each = NEW_CAP // N_SHARD
    keys = jax.random.split(key, 3)
    heavy_col = jax.random.randint(keys[0], (), 0, count)
    columns = jnp.arange(count, dtype=jnp.int32)
    is_heavy = columns[None, :] == heavy_col
    remaining = OLD_ROWS - each
    scores = jax.random.randint(keys[1], (count, count), 0, 1 << 20) * count + columns[None, :]
    scores = jnp.where(is_heavy, 1 << 30, scores)
    ordering = jnp.argsort(scores, axis=1, stable=True)
    position = jnp.argsort(ordering, axis=1, stable=True)
    share = remaining // (count - 1)
    surplus = remaining % (count - 1)
    counts = share + (position < surplus).astype(jnp.int32)
    counts = jnp.where(is_heavy, each, counts).astype(jnp.int32)
    for turn in range(8):
        round_key = jax.random.fold_in(keys[2], turn)
        pair_key, delta_key = jax.random.split(round_key)
        pairing = jax.random.permutation(pair_key, count)
        left = pairing[0::2]
        right = pairing[1::2]
        first_side = counts[:, left]
        second_side = counts[:, right]
        lower = -jnp.minimum(second_side, each - first_side)
        upper = jnp.minimum(first_side, each - second_side)
        frozen = (left == heavy_col) | (right == heavy_col)
        moved = jax.random.randint(delta_key, first_side.shape, lower, upper + 1)
        moved = jnp.where(frozen[None, :], 0, moved)
        counts = counts.at[:, left].set(first_side - moved).at[:, right].set(second_side + moved)
    return counts


def plan_blocks(key):
    counts = plan_counts(jax.random.fold_in(key, 11))
    order_scores = jax.random.randint(jax.random.fold_in(key, 23), (N_SHARD, N_SHARD), 0, 1 << 20) * N_SHARD + jnp.arange(N_SHARD, dtype=jnp.int32)[None, :]
    owners = jnp.argsort(order_scores, axis=1, stable=True).astype(jnp.int32)
    sizes = jnp.take_along_axis(counts, owners, axis=1).astype(jnp.int32)
    return (owners, sizes)


def draw_segment_fresh_owner(key, part):
    return plan_blocks(key)[0]


def draw_segment_line_lengths(key, part):
    return plan_blocks(key)[1]


def block_levels(rng, dims, cuts, smallest, high):
    level, own = 1.0, jax.random.fold_in(rng, 6)
    for dim, blocks in cuts:
        draws = jnp.exp(jax.random.uniform(jax.random.fold_in(own, dim), (blocks,), jnp.float32, smallest / len(cuts), high / len(cuts)))
        level = level * jnp.repeat(draws, dims[dim] // blocks).reshape([-1 if axis == dim else 1 for axis in range(len(dims))])
    return level


def normal_values(rng, dims, scale, most, cuts=(), kind=jnp.bfloat16):
    gain = block_levels(rng, dims, cuts, -0.22, 0.18) if cuts else 1.0
    drawn = jax.random.normal(rng, dims, jnp.float32) * scale * gain
    return jnp.minimum(jnp.maximum(drawn, -most), most).astype(kind)


def setup_inputs(seed: int = 0) -> dict:
    key_list = jax.random.split(jax.random.key(seed), 8)
    return {
        "earlier_precise_parameters": normal_values(key_list[0], (GROUPS, N_SHARD * OLD_ROWS, ROW_VALUES), 1.0, 6.0, ((0, 8), (1, 4)), jnp.float32),
        "earlier_mean_estimate": normal_values(key_list[1], (GROUPS, N_SHARD * OLD_ROWS, ROW_VALUES), 1.0, 6.0, ((0, 8), (1, 4)), jnp.float32),
        "earlier_variance_estimate": jnp.clip(jnp.exp(math.log(10.0) - 6.9077553 * jax.random.uniform(key_list[2], (GROUPS, N_SHARD * OLD_ROWS, ROW_VALUES), jnp.float32) ** block_levels(key_list[2], (GROUPS, N_SHARD * OLD_ROWS, ROW_VALUES), ((0, 8), (1, 4)), -0.2, 0.2)), 0.01, 10.0),
        "replica_slope_portions": normal_values(key_list[3], (GROUPS, N_SHARD * GROUPS * NEW_CAP, ROW_VALUES), 1.0, 6.0, ((0, 8), (1, 4))),
        "segment_fresh_owner": draw_segment_fresh_owner(jax.random.fold_in(key_list[7], 71), 0),
        "segment_line_lengths": draw_segment_line_lengths(jax.random.fold_in(key_list[7], 71), 0),
        "remaining_worker": jax.random.permutation(key_list[6], N_SHARD).astype(jnp.int32),
    }


beta_first = 0.9
beta_second = 0.95
bias_first = 1.0 - 0.9 ** 50
bias_second = 1.0 - 0.95 ** 50
epsilon_adam = 1e-08
decay_rate = 0.1
learn_rate = 0.0003

def block_tables(segment_fresh_owner, segment_line_lengths, shard_count):
    block_starts = (jnp.cumsum(segment_line_lengths, axis=1) - segment_line_lengths).astype(jnp.int32)
    peers = jnp.arange(shard_count, dtype=jnp.int32)
    pair_rows = lax.optimization_barrier(jnp.sum(jnp.where(segment_fresh_owner[:, :, None] == peers[None, None, :], segment_line_lengths[:, :, None], 0), axis=1)).astype(jnp.int32)
    pair_offset = (jnp.cumsum(pair_rows, axis=0) - pair_rows).astype(jnp.int32)
    return (block_starts, pair_rows, pair_offset)

def locate_rows(ranks, inner, segment_fresh_owner, segment_line_lengths, block_starts):
    rank_starts = block_starts[ranks]
    rank_ends = rank_starts + segment_line_lengths[ranks]
    block_index = lax.optimization_barrier(jnp.sum((rank_ends <= inner[:, None]).astype(jnp.int32), axis=1)).astype(jnp.int32)
    owner = jnp.take_along_axis(segment_fresh_owner[ranks], block_index[:, None], axis=1)[:, 0]
    offset = inner - jnp.take_along_axis(rank_starts, block_index[:, None], axis=1)[:, 0]
    return (owner.astype(jnp.int32), offset.astype(jnp.int32))

def adam_update(weights, first, squares, gradient, live):
    moment = beta_first * first + (1.0 - beta_first) * gradient
    second = beta_second * squares + (1.0 - beta_second) * gradient * gradient
    update = moment / bias_first / (jnp.sqrt(second / bias_second) + epsilon_adam) + decay_rate * weights
    new_weights = weights - learn_rate * update
    keep = live.astype(jnp.float32)[:, None]
    return (new_weights * keep, moment * keep, second * keep)

def reference(earlier_precise_parameters, earlier_mean_estimate, earlier_variance_estimate, replica_slope_portions, segment_fresh_owner, segment_line_lengths, remaining_worker):
    width = ROW_VALUES
    keeping_worker = jnp.zeros((N_SHARD,), jnp.int32).at[remaining_worker].set(jnp.arange(N_SHARD, dtype=jnp.int32))
    stacked = jnp.concatenate([earlier_precise_parameters, earlier_mean_estimate, earlier_variance_estimate], axis=2)
    by_rank = stacked.reshape(GROUPS, N_SHARD, OLD_ROWS, 3 * width)[:, keeping_worker]
    by_rank = by_rank.reshape(GROUPS, N_SHARD * OLD_ROWS, 3 * width)
    block_starts, pair_rows, pair_offset = block_tables(segment_fresh_owner, segment_line_lengths, N_SHARD)
    ranks = jnp.repeat(jnp.arange(N_SHARD, dtype=jnp.int32), OLD_ROWS)
    inner = jnp.tile(jnp.arange(OLD_ROWS, dtype=jnp.int32), N_SHARD)
    owner, offset = locate_rows(ranks, inner, segment_fresh_owner, segment_line_lengths, block_starts)
    target = owner * NEW_CAP + pair_offset[ranks, owner] + offset
    placed = jnp.zeros((GROUPS, N_SHARD * NEW_CAP, 3 * width), jnp.float32).at[:, target].set(by_rank)
    totals = lax.optimization_barrier(jnp.sum(pair_rows, axis=0)).astype(jnp.int32)
    live = (jnp.arange(NEW_CAP, dtype=jnp.int32)[None, :] < totals[:, None]).reshape(N_SHARD * NEW_CAP)

    def accumulate(total, part):
        return (total + part.astype(jnp.float32), None)
    summed, unused = lax.scan(accumulate, jnp.zeros((N_SHARD * GROUPS * NEW_CAP, width), jnp.float32), replica_slope_portions)
    gradient = summed.reshape(N_SHARD, GROUPS, NEW_CAP, width).transpose(1, 0, 2, 3).reshape(GROUPS, N_SHARD * NEW_CAP, width)
    weights = placed[:, :, :width]
    first = placed[:, :, width:2 * width]
    squares = placed[:, :, 2 * width:]
    return adam_update(weights, first, squares, gradient, live)
```

```python
import functools

import jax
import jax.numpy as jnp
from jax import lax
from jax.experimental import pallas as pl
from jax.experimental.pallas import tpu as pltpu
from jax.sharding import PartitionSpec as P

beta_first = 0.9
beta_second = 0.95
bias_first = 1.0 - 0.9**50
bias_second = 1.0 - 0.95**50
epsilon_adam = 1e-08
decay_rate = 0.1
learn_rate = 0.0003

DIRECT_PEERS = 8
PARAMS = pltpu.CompilerParams(vmem_limit_bytes=16 * 2**20)

VMEM = pl.BlockSpec(memory_space=pltpu.VMEM)
SMEM = pl.BlockSpec(memory_space=pltpu.SMEM)


def peer(index, turn, count):
    return index ^ turn if count & (count - 1) == 0 else lax.rem(index + turn, count)


def origin(index, turn, count):
    return index ^ turn if count & (count - 1) == 0 else lax.rem(index + count - turn, count)


def route(turn, count):
    if count & (count - 1) == 0:
        return [(i, i ^ turn) for i in range(count)]
    return [(i, (i + turn) % count) for i in range(count)]


def exchange(value, axis, turn):
    return lax.ppermute(value, axis, route(turn, lax.axis_size(axis)))


def loop(count, body):
    if count <= DIRECT_PEERS:
        for step in range(count):
            body(step)
    else:
        lax.fori_loop(0, count, lambda step, _: (body(step), 0)[1], 0)


def pack_kernel(count, slot, owner, lengths, worker, w, m, v, *rest):
    outs, (padded, starts) = rest[:-2], rest[-2:]
    rows = w.shape[1]
    me = lax.axis_index("shard")
    rank = worker[me]

    def place(block, start):
        starts[owner[rank, block]] = start
        return start + lengths[rank, block]

    start = jnp.int32(0)
    if count <= DIRECT_PEERS:
        for block in range(count):
            start = place(block, start)
    else:
        lax.fori_loop(0, count, place, start)
    for part, ref in enumerate((w, m, v)):
        padded[part, pl.ds(0, rows), :] = ref[0]
        padded[part, pl.ds(rows, padded.shape[1] - rows), :] = jnp.zeros(
            (padded.shape[1] - rows, ref.shape[2]), jnp.float32
        )
    if len(outs) == count:
        for turn in range(count):
            first = starts[peer(me, turn, count)]
            for part in range(3):
                outs[turn][part] = padded[part, pl.ds(first, slot), :]
    else:

        def fill(dest):
            first = starts[dest]
            for part in range(3):
                outs[0][dest, part] = padded[part, pl.ds(first, slot), :]

        loop(count, fill)


def pack(count, slot, owner, lengths, worker, w, m, v):
    rows, width = w.shape[1:]
    direct = count <= DIRECT_PEERS
    shape = (3, slot, width)
    out = [jax.ShapeDtypeStruct(shape, jnp.float32)] * count if direct else [jax.ShapeDtypeStruct((count,) + shape, jnp.float32)]
    return pl.pallas_call(
        functools.partial(pack_kernel, count, slot),
        out_shape=out,
        in_specs=[SMEM] * 3 + [VMEM] * 3,
        out_specs=[VMEM] * len(out),
        scratch_shapes=[
            pltpu.VMEM((3, rows + max(slot, 8), width), jnp.float32),
            pltpu.SMEM((count,), jnp.int32),
        ],
        compiler_params=PARAMS,
        name="pack",
    )(owner, lengths, worker, w, m, v)


def widen_kernel(reps, grads, *outs):
    me = lax.axis_index("rep")
    for turn in range(1, reps):
        theirs = peer(me, turn, reps)
        for block in range(grads.shape[0]):
            outs[turn - 1][block] = grads[block, theirs].astype(jnp.float32)


def widen(reps, grads):
    blocks, _, rows, width = grads.shape
    return pl.pallas_call(
        functools.partial(widen_kernel, reps),
        out_shape=[jax.ShapeDtypeStruct((blocks, rows, width), jnp.float32)] * (reps - 1),
        in_specs=[VMEM],
        out_specs=[VMEM] * (reps - 1),
        compiler_params=PARAMS,
        name="widen",
    )(grads)


def fold_kernel(reps, count, grads, *refs):
    arrived, outs = refs[: reps - 1], refs[reps - 1 :]
    rep = lax.axis_index("rep")
    me = lax.axis_index("dp")
    for turn in range(count):
        block = peer(me, turn, count)
        total = grads[block, rep].astype(jnp.float32)
        for ref in arrived:
            total += ref[block]
        outs[turn][...] = total


def fold(reps, grads, arrived):
    count, _, rows, width = grads.shape
    return pl.pallas_call(
        functools.partial(fold_kernel, reps, count),
        out_shape=[jax.ShapeDtypeStruct((rows, width), jnp.float32)] * count,
        in_specs=[VMEM] * reps,
        out_specs=[VMEM] * count,
        compiler_params=PARAMS,
        name="fold",
    )(grads, *arrived)


def adam_kernel(count, parts, slot, owner, lengths, worker, *refs):
    n_chunks = count if count <= DIRECT_PEERS else 1
    chunks = refs[:n_chunks]
    sums = refs[n_chunks : n_chunks + parts]
    new_w, new_m, new_v, placed, where = refs[n_chunks + parts :]
    capacity = new_w.shape[1]
    me = lax.axis_index("shard")

    def locate(position):
        where[worker[position]] = position

    loop(count, locate)

    def rows_of(rank):
        if count <= DIRECT_PEERS:
            total = jnp.int32(0)
            for block in range(count):
                total += jnp.where(owner[rank, block] == me, lengths[rank, block], 0)
            return total
        return lax.fori_loop(
            0, count, lambda b, t: t + jnp.where(owner[rank, b] == me, lengths[rank, b], 0), jnp.int32(0)
        )

    if count <= DIRECT_PEERS:
        total = jnp.int32(0)
        for rank in range(count):
            source = where[rank]
            for turn in range(count):

                @pl.when(origin(me, turn, count) == source)
                def _():
                    for part in range(3):
                        placed[part, pl.ds(total, slot), :] = chunks[turn][part]

            total += rows_of(rank)
    else:

        def put(rank, total):
            for part in range(3):
                placed[part, pl.ds(total, slot), :] = chunks[0][where[rank], part]
            return total + rows_of(rank)

        total = lax.fori_loop(0, count, put, jnp.int32(0))

    gradient = sums[0][...]
    for ref in sums[1:]:
        gradient += ref[...]
    live = lax.broadcasted_iota(jnp.int32, gradient.shape, 0) < total
    weights = placed[0, :capacity, :]
    moment = beta_first * placed[1, :capacity, :] + (1.0 - beta_first) * gradient
    second = beta_second * placed[2, :capacity, :] + (1.0 - beta_second) * gradient * gradient
    update = (
        moment / bias_first / (jnp.sqrt(second / bias_second) + epsilon_adam) + decay_rate * weights
    )
    new_w[0] = jnp.where(live, weights - learn_rate * update, 0.0)
    new_m[0] = jnp.where(live, moment, 0.0)
    new_v[0] = jnp.where(live, second, 0.0)


def adam(count, slot, owner, lengths, worker, chunks, sums):
    capacity, width = sums[0].shape
    out = jax.ShapeDtypeStruct((1, capacity, width), jnp.float32)
    return pl.pallas_call(
        functools.partial(adam_kernel, count, len(sums), slot),
        out_shape=[out] * 3,
        in_specs=[SMEM] * 3 + [VMEM] * (len(chunks) + len(sums)),
        out_specs=[VMEM] * 3,
        scratch_shapes=[
            pltpu.VMEM((3, capacity + max(slot, 8), width), jnp.float32),
            pltpu.SMEM((count,), jnp.int32),
        ],
        compiler_params=PARAMS,
        name="adam",
    )(owner, lengths, worker, *chunks, *sums)


def local(w, m, v, portions, owner, lengths, worker):
    shards = lax.axis_size("shard")
    groups = lax.axis_size("dp")
    reps = lax.axis_size("rep")
    capacity = portions.shape[1] // (groups * reps)
    slot = capacity // shards
    grads = portions.reshape(groups, reps, capacity, portions.shape[2])

    halves = widen(reps, grads)
    arrived = [exchange(halves[t - 1], "rep", t) for t in range(1, reps)]
    packed = pack(shards, slot, owner, lengths, worker, w, m, v)
    if shards <= DIRECT_PEERS:
        chunks = [packed[0]] + [exchange(packed[t], "shard", t) for t in range(1, shards)]
    else:
        chunks = [lax.all_to_all(packed[0], "shard", 0, 0, tiled=True)]
    folded = fold(reps, grads, arrived)
    sums = [folded[0]] + [exchange(folded[t], "dp", t) for t in range(1, groups)]
    return tuple(adam(shards, slot, owner, lengths, worker, chunks, sums))


def solution(mesh):
    split = P(("dp", "rep"), "shard", None)
    return jax.shard_map(
        local,
        mesh=mesh,
        in_specs=(split,) * 4 + (P(),) * 3,
        out_specs=(split,) * 3,
        check_vma=False,
    )
```
